32 devices in a mesh: outer: 8 (over y, x, core), inner: 4 (over z).
Axes of the slice: x: 2, y: 2, z: 4, core: 2. Of those that a mesh axis runs over, the one named last changes fastest.
Arguments:
- leaf_fronts: float32 [32, 512, 512], P(('outer', 'inner')), as said below
- pivot_count: int32 [32], P(('outer', 'inner')), may hold values from 64 to 256, as said below
- update_rows: int32 [32, 256], P(('outer', 'inner')), may hold values from 0 to 8191, as said below
- top_front: float32 [8192, 8192], P('outer', 'inner'), as said below
Outputs:
- factor: float32 [8192, 128], P('outer')
- schur: float32 [8192, 8192], P('outer', 'inner')
The draws below stay inside these ranges and needn't reach their ends.
Inputs may be any that keep to these rules, and one draw needn't show every extreme that they name: `pivot_count`: a multiple of 64; both ends occur. `update_rows`: each row strictly increases and holds exactly 32 entries in each block of 1024 consecutive top front rows. `leaf_fronts`: each front is symmetric positive definite. `top_front`: symmetric positive definite.
All inputs are finite; a program needn't handle non-finite values.
Results may differ from the reference program's by a relative error of at most 0.0003.
Values sent between devices are 32-bit elements; how exact they have to be, the bound alone decides.
A program may use at most 64 MiB of HBM per device.

```python
import math
import jax
import jax.numpy as jnp
from jax import lax

NT = 8192
PV = 256
U = 256
PIV = 128
FR = 512
TILE_ROWS = 1024
PER_BLOCK = 32
N_OUTER = 8
DEVICES = 32


leaf_length = 0.2


top_length = 0.5


top_weight = 4.0


def spread_draw(key, shape, lower, upper):
    return jnp.exp(jax.random.uniform(key, shape, jnp.float32, math.log(lower), math.log(upper)))


def kernel_front(key, order, length):
    points = jax.random.uniform(jax.random.fold_in(key, 1), (order, 3), jnp.float32)
    nugget = spread_draw(jax.random.fold_in(key, 2), (order,), 0.5, 2.0)
    row_scale = spread_draw(jax.random.fold_in(key, 3), (order,), 0.7, 1.4)
    first = points[:, None, 0] - points[None, :, 0]
    second = points[:, None, 1] - points[None, :, 1]
    third = points[:, None, 2] - points[None, :, 2]
    distance = jnp.sqrt(first * first + second * second + third * third)
    kernel = jnp.exp(-distance / length) + jnp.diag(nugget)
    scales = row_scale[:, None] * row_scale[None, :]
    return kernel * scales


def draw_leaf_fronts(key, part):
    front_keys = jax.random.split(key, DEVICES)

    def one_front(front_key):
        front_scale = spread_draw(jax.random.fold_in(front_key, 4), (), 0.5, 2.0)
        return kernel_front(front_key, FR, leaf_length) * front_scale
    return lax.map(one_front, front_keys).astype(jnp.float32)


def draw_top_front(key, part):
    return (kernel_front(key, NT, top_length) * top_weight).astype(jnp.float32)


def draw_pivot_count(key, part):
    levels = jax.random.randint(key, (DEVICES,), 1, 5)
    levels = levels.at[0].set(4).at[1].set(1)
    return (levels * (PV // 4)).astype(jnp.int32)


def draw_update_rows(key, part):
    scores = jax.random.randint(key, (DEVICES, N_OUTER, TILE_ROWS), 0, 2 ** 20)
    scores = scores * TILE_ROWS + jnp.arange(TILE_ROWS, dtype=jnp.int32)[None, None, :]
    chosen = jnp.argsort(scores, axis=-1)[:, :, :PER_BLOCK].astype(jnp.int32)
    chosen = jnp.sort(chosen, axis=-1)
    offsets = jnp.arange(N_OUTER, dtype=jnp.int32)[None, :, None] * TILE_ROWS
    return (chosen + offsets).reshape(DEVICES, U).astype(jnp.int32)


def setup_inputs(seed: int = 0) -> dict:
    splits = jax.random.split(jax.random.key(seed), 5)
    return {
        "leaf_fronts": draw_leaf_fronts(jax.random.fold_in(splits[4], 71), 0),
        "pivot_count": draw_pivot_count(jax.random.fold_in(splits[4], 71), 0),
        "update_rows": draw_update_rows(jax.random.fold_in(splits[4], 71), 0),
        "top_front": draw_top_front(jax.random.fold_in(splits[4], 71), 0),
    }


def leaf_update(front_matrix, pivots):
    kept_mask = jnp.arange(PV) < pivots
    both_kept = kept_mask[:, None] & kept_mask[None, :]
    pivot_block = jnp.where(both_kept, front_matrix[:PV, :PV], 0.0) + jnp.diag(jnp.where(kept_mask, 0.0, 1.0))
    coupling = jnp.where(kept_mask[None, :], front_matrix[PV:, :PV], 0.0)
    pivot_chol = jnp.linalg.cholesky(pivot_block)
    scaled_coupling = lax.linalg.triangular_solve(pivot_chol, coupling, left_side=False, lower=True, transpose_a=True)
    return front_matrix[PV:, PV:] - jnp.dot(scaled_coupling, scaled_coupling.T, precision=lax.Precision.HIGHEST)

def reference(leaf_fronts, pivot_count, update_rows, top_front):

    def absorb(assembled, leaf_item):
        front_matrix, pivots, target_rows = leaf_item
        update = leaf_update(front_matrix, pivots)
        assembled = assembled.at[target_rows[:, None], target_rows[None, :]].add(update)
        return (assembled, None)
    assembled, unused = lax.scan(absorb, top_front, (leaf_fronts, pivot_count, update_rows))
    lead = jnp.linalg.cholesky(assembled[:PIV, :PIV])
    factor = lax.linalg.triangular_solve(lead, assembled[:, :PIV], left_side=False, lower=True, transpose_a=True)
    factor = jnp.where(jnp.arange(NT)[:, None] >= jnp.arange(PIV)[None, :], factor, 0.0)
    trailing = assembled[PIV:, PIV:] - jnp.dot(factor[PIV:], factor[PIV:].T, precision=lax.Precision.HIGHEST)
    schur = jnp.zeros((NT, NT), jnp.float32).at[PIV:, PIV:].set(trailing)
    return (factor, schur)
```

```python
import functools

import jax
import jax.numpy as jnp
from jax import lax
from jax.experimental import pallas as pl
from jax.experimental.pallas import tpu as pltpu
from jax.sharding import PartitionSpec as P

PV = 256
U = 256
PIV = 128
NB = 64
AXES = ("outer", "inner")


def iota(shape, dim):
    return lax.broadcasted_iota(jnp.int32, shape, dim)


def dot(a, b, ca=1, cb=0):
    return lax.dot_general(
        a, b, (((ca,), (cb,)), ((), ())), preferred_element_type=jnp.float32
    )


def halves(x):
    high = x.astype(jnp.bfloat16)
    return high, (x - high.astype(jnp.float32)).astype(jnp.bfloat16)


def dot3(a, b, ca=1, cb=0):
    a_high, a_low = halves(a)
    b_high, b_low = halves(b)
    return dot(a_high, b_high, ca, cb) + (dot(a_high, b_low, ca, cb) + dot(a_low, b_high, ca, cb))


def dot6(a, b, ca=1, cb=0):
    return lax.dot_general(
        a,
        b,
        (((ca,), (cb,)), ((), ())),
        precision=lax.Precision.HIGHEST,
        preferred_element_type=jnp.float32,
    )


def inverse_cholesky(block):
    order = block.shape[0]
    unit = (iota((order, order), 0) == iota((order, order), 1)).astype(jnp.float32)
    joined = jnp.concatenate([block, unit], axis=1)
    width = joined.shape[1]
    count = order // 8
    rows = [joined[8 * b : 8 * b + 8] for b in range(count)]
    sub = iota((8, width), 0)
    scales = []
    for k in range(count):
        cols = {
            b: [
                jnp.broadcast_to(rows[b][:, 8 * k + j : 8 * k + j + 1], (8, width))
                for j in range(8)
            ]
            for b in range(k, count)
        }
        scale = jnp.zeros((8, width), jnp.float32)
        for j in range(8):
            pivot = jnp.broadcast_to(cols[k][j][j : j + 1], (8, width))
            inverse = 1.0 / pivot
            scale = jnp.where(sub == j, lax.rsqrt(pivot), scale)
            row = jnp.broadcast_to(rows[k][j : j + 1], (8, width))
            heads = [jnp.broadcast_to(cols[k][l][j : j + 1], (8, width)) for l in range(8)]
            for b in range(k, count):
                weight = cols[b][j] * inverse
                if b == k:
                    weight = jnp.where(sub > j, weight, 0.0)
                rows[b] = rows[b] - weight * row
                for l in range(j + 1, 8):
                    cols[b][l] = cols[b][l] - weight * heads[l]
        scales.append(scale)
    scaled = jnp.concatenate([rows[b] * scales[b] for b in range(count)], axis=0)
    return scaled[:, order:]


def leaf_kernel(n_outer, n_inner, pivots_ref, front_ref, panel_ref, tile_ref, work):
    live = pivots_ref[0]
    row = iota((PV, PV + U), 0)
    col = iota((PV, PV + U), 1)
    keep = (row < live) & ((col < live) | (col >= PV))
    unit = jnp.where((row == col) & (row >= live), 1.0, 0.0)
    work[...] = jnp.where(keep, front_ref[0, :PV, :], unit)
    for start in range(0, PV, NB):
        stop = start + NB
        inverse = inverse_cholesky(work[start:stop, start:stop])
        solved = dot6(inverse, work[start:stop, :])
        work[start:stop, :] = solved
        if stop < PV:
            work[stop:, :] = work[stop:, :] - dot6(solved[:, stop:PV], solved, 0, 0)
    coupling = work[:, PV:]
    update = front_ref[0, PV:, PV:] - dot6(coupling, coupling, 0, 0)
    per_row, per_col = U // n_outer, U // n_inner
    half = per_row // 2
    lead = update[:per_row]
    for o in range(n_outer):
        for i in range(n_inner):
            columns = slice(i * per_col, (i + 1) * per_col)
            panel_ref[o * n_inner + i] = jnp.concatenate(
                [
                    lead[:, :per_row],
                    lead[:, columns],
                    lead[:, o * per_row : (o + 1) * per_row],
                ],
                axis=1,
            )
            first = o * per_row
            tile_ref[o * n_inner + i] = jnp.concatenate(
                [
                    update[first : first + half, columns],
                    update[first + half : first + per_row, columns],
                ],
                axis=1,
            )


def panel_kernel(
    shape,
    panel_ref,
    lead_lane,
    lead_sub,
    row_sub,
    col_sub,
    pivot_ref,
    slab_ref,
    columns_ref,
    factor_ref,
    slab_factor_ref,
    e_pivot,
    e_slab,
    e_row,
):
    leaves, per_row, per_col, tile_rows, tile_cols = shape
    for d in range(leaves):
        lanes = lead_lane[:, d * per_row : (d + 1) * per_row]
        pick = (iota((PIV, per_row), 0) == lanes).astype(jnp.bfloat16)
        high, low = halves(panel_ref[d])
        spread = dot(pick, high) + dot(pick, low)
        e_pivot[:, d * per_row : (d + 1) * per_row] = spread[:, :per_row]
        e_slab[:, d * per_col : (d + 1) * per_col] = spread[:, per_row : per_row + per_col]
        e_row[:, d * per_row : (d + 1) * per_row] = spread[:, per_row + per_col :]

    def place(source, index_ref, width):
        depth = source.shape[1]
        pick = (iota((depth, width), 1) == index_ref[...]).astype(jnp.bfloat16)
        high, low = halves(source)
        return dot(high, pick) + dot(low, pick)

    pivot = pivot_ref[...] + place(e_pivot[...], lead_sub, PIV)
    first = inverse_cholesky(pivot[:NB, :NB])
    across = dot6(first, pivot[:NB, NB:])
    second = inverse_cholesky(pivot[NB:, NB:] - dot6(across, across, 0, 0))
    below = -dot6(second, dot6(across, first, 0, 0))
    inverse = jnp.concatenate(
        [
            jnp.concatenate([first, jnp.zeros_like(first)], axis=1),
            jnp.concatenate([below, second], axis=1),
        ],
        axis=0,
    )
    width = min(tile_cols, 512)
    for start in range(0, tile_cols, width):
        pick = (iota((leaves * per_col, width), 1) + start == col_sub[...]).astype(jnp.bfloat16)
        high, low = halves(e_slab[...])
        part = slab_ref[:, start : start + width] + (dot(high, pick) + dot(low, pick))
        slab_factor_ref[:, start : start + width] = dot3(inverse, part)
    width = min(tile_rows, 512)
    for start in range(0, tile_rows, width):
        pick = (iota((leaves * per_row, width), 1) + start == row_sub[...]).astype(jnp.bfloat16)
        high, low = halves(e_row[...])
        part = columns_ref[start : start + width, :].T + (dot(high, pick) + dot(low, pick))
        factor_ref[start : start + width, :] = dot3(inverse, part).T

    outer_index = lax.axis_index("outer")

    @pl.when(outer_index * tile_rows < PIV)
    def _():
        for start in range(0, tile_rows, 128):
            span = min(128, tile_rows - start)
            rows = outer_index * tile_rows + start + iota((span, PIV), 0)
            block = factor_ref[start : start + span, :]
            factor_ref[start : start + span, :] = jnp.where(
                rows >= iota((span, PIV), 1), block, 0.0
            )


def trailing_kernel(
    shape, tile_ref, row_lane, col_sub, top_ref, factor_ref, slab_ref, schur_ref, high_ref, low_ref
):
    leaves, per_row, per_col, tile_rows, tile_cols = shape
    step = pl.program_id(0)
    height = top_ref.shape[0]
    half = per_row // 2

    @pl.when(step == 0)
    def _():
        for d in range(leaves):
            packed = tile_ref[d]
            values = jnp.concatenate([packed[:, :per_col], packed[:, per_col:]], axis=0)
            pick = (
                iota((per_col, tile_cols), 1) == col_sub[d * per_col : (d + 1) * per_col, :]
            ).astype(jnp.bfloat16)
            high, low = halves(values)
            spread = dot(high, pick)
            spread_low = dot(low, pick)
            high_ref[d * per_row : (d + 1) * per_row, :] = spread.astype(jnp.bfloat16)
            low_ref[d * per_row : (d + 1) * per_row, :] = spread_low.astype(jnp.bfloat16)

    rows = step * height + iota((height, leaves * per_row), 0)
    pick = (rows == row_lane[...]).astype(jnp.bfloat16)
    f_high, f_low = halves(-factor_ref[...])
    width = min(tile_cols, 512)
    row_global = lax.axis_index("outer") * tile_rows + step * height + iota((height, width), 0)
    for start in range(0, tile_cols, width):
        cols = slice(start, start + width)
        s_high, s_low = halves(slab_ref[:, cols])
        total = dot(pick, high_ref[:, cols]) + dot(pick, low_ref[:, cols])
        total = total + (dot(f_high, s_high) + (dot(f_high, s_low) + dot(f_low, s_high)))
        col_global = lax.axis_index("inner") * tile_cols + start + iota((height, width), 1)
        keep = (row_global >= PIV) & (col_global >= PIV)
        schur_ref[:, cols] = jnp.where(keep, top_ref[:, cols] + total, 0.0)


def shards(leaf_fronts, pivot_count, update_rows, top_front):
    n_outer = lax.axis_size("outer")
    n_inner = lax.axis_size("inner")
    outer_index = lax.axis_index("outer")
    inner_index = lax.axis_index("inner")
    tile_rows, tile_cols = top_front.shape
    leaves = n_outer * n_inner
    per_row, per_col = U // n_outer, U // n_inner
    shape = (leaves, per_row, per_col, tile_rows, tile_cols)
    vmem = pl.BlockSpec(memory_space=pltpu.VMEM)
    big = pltpu.CompilerParams(vmem_limit_bytes=56 << 20)

    def spread(block, axis, index, count, stride):
        total = jnp.where(index == 0, block, 0.0)
        for target in range(stride, count, stride):
            total = total + lax.ppermute(block, axis, [(0, target)])
        for gap in range(1, stride):
            near = [(start, start + gap) for start in range(0, count, stride)]
            total = jnp.where(index % stride == gap, lax.ppermute(total, axis, near), total)
        return total

    slab = spread(top_front[:PIV, :], "outer", outer_index, n_outer, 2)
    columns = spread(top_front[:, :PIV], "inner", inner_index, n_inner, 1)
    pivot_raw = spread(slab[:, :PIV], "inner", inner_index, n_inner, 1)

    indices = lax.all_to_all(
        jnp.broadcast_to(update_rows, (leaves, U)), AXES, split_axis=0, concat_axis=0, tiled=True
    )

    panel, tiles = pl.pallas_call(
        functools.partial(leaf_kernel, n_outer, n_inner),
        out_shape=(
            jax.ShapeDtypeStruct((leaves, per_row, 2 * per_row + per_col), jnp.float32),
            jax.ShapeDtypeStruct((leaves, per_row // 2, 2 * per_col), jnp.float32),
        ),
        in_specs=[pl.BlockSpec(memory_space=pltpu.SMEM), vmem],
        out_specs=(vmem, vmem),
        scratch_shapes=[pltpu.VMEM((PV, PV + U), jnp.float32)],
        compiler_params=big,
        cost_estimate=pl.CostEstimate(
            flops=20_000_000_000, bytes_accessed=3_000_000, transcendentals=0
        ),
    )(pivot_count, leaf_fronts)

    def exchange(x):
        return lax.all_to_all(x, AXES, split_axis=0, concat_axis=0, tiled=True)

    panel = exchange(panel)
    tiles = exchange(tiles)

    lead = indices[:, :per_row].reshape(-1)
    rows = lax.dynamic_slice_in_dim(indices, outer_index * per_row, per_row, 1) % tile_rows
    cols = lax.dynamic_slice_in_dim(indices, inner_index * per_col, per_col, 1) % tile_cols
    col_sub = cols.reshape(-1, 1)
    row_flat = rows.reshape(-1)

    factor, slab_factor = pl.pallas_call(
        functools.partial(panel_kernel, shape),
        out_shape=(
            jax.ShapeDtypeStruct((tile_rows, PIV), jnp.float32),
            jax.ShapeDtypeStruct((PIV, tile_cols), jnp.float32),
        ),
        in_specs=[vmem] * 8,
        out_specs=(vmem, vmem),
        scratch_shapes=[
            pltpu.VMEM((PIV, leaves * per_row), jnp.float32),
            pltpu.VMEM((PIV, leaves * per_col), jnp.float32),
            pltpu.VMEM((PIV, leaves * per_row), jnp.float32),
        ],
        compiler_params=big,
    )(
        panel,
        lead.reshape(1, -1),
        lead.reshape(-1, 1),
        row_flat.reshape(-1, 1),
        col_sub,
        pivot_raw,
        slab,
        columns,
    )

    height = min(tile_rows, 128)
    whole = lambda *dims: pl.BlockSpec(dims, lambda r: (0,) * len(dims))
    schur = pl.pallas_call(
        functools.partial(trailing_kernel, shape),
        out_shape=jax.ShapeDtypeStruct((tile_rows, tile_cols), jnp.float32),
        grid=(tile_rows // height,),
        in_specs=[
            whole(leaves, per_row // 2, 2 * per_col),
            whole(1, leaves * per_row),
            whole(leaves * per_col, 1),
            pl.BlockSpec((height, tile_cols), lambda r: (r, 0)),
            pl.BlockSpec((height, PIV), lambda r: (r, 0)),
            whole(PIV, tile_cols),
        ],
        out_specs=pl.BlockSpec((height, tile_cols), lambda r: (r, 0)),
        scratch_shapes=[
            pltpu.VMEM((leaves * per_row, tile_cols), jnp.bfloat16),
            pltpu.VMEM((leaves * per_row, tile_cols), jnp.bfloat16),
        ],
        compiler_params=big,
    )(tiles, row_flat.reshape(1, -1), col_sub, top_front, factor, slab_factor)
    return (factor, schur)


def solution(mesh):
    placed = (
        P(("outer", "inner"), None, None),
        P(("outer", "inner")),
        P(("outer", "inner"), None),
        P("outer", "inner"),
    )
    return jax.shard_map(
        shards,
        mesh=mesh,
        in_specs=placed,
        out_specs=(P("outer", None), P("outer", "inner")),
        check_vma=False,
    )
```

```python
import functools

import jax
import jax.numpy as jnp
from jax import lax
from jax.experimental import pallas as pl
from jax.experimental.pallas import tpu as pltpu
from jax.sharding import PartitionSpec as P

PV = 256
U = 256
PIV = 128
NB = 64


def iota(shape, dim):
    return lax.broadcasted_iota(jnp.int32, shape, dim)


def dot(a, b, ca=1, cb=0):
    return lax.dot_general(
        a, b, (((ca,), (cb,)), ((), ())), preferred_element_type=jnp.float32
    )


def halves(x):
    high = x.astype(jnp.bfloat16)
    return high, (x - high.astype(jnp.float32)).astype(jnp.bfloat16)


def dot3(a, b, ca=1, cb=0):
    a_high, a_low = halves(a)
    b_high, b_low = halves(b)
    return dot(a_high, b_high, ca, cb) + (dot(a_high, b_low, ca, cb) + dot(a_low, b_high, ca, cb))


def dot6(a, b, ca=1, cb=0):
    return lax.dot_general(
        a,
        b,
        (((ca,), (cb,)), ((), ())),
        precision=lax.Precision.HIGHEST,
        preferred_element_type=jnp.float32,
    )


def inverse_cholesky(block):
    order = block.shape[0]
    unit = (iota((order, order), 0) == iota((order, order), 1)).astype(jnp.float32)
    joined = jnp.concatenate([block, unit], axis=1)
    width = joined.shape[1]
    count = order // 8
    rows = [joined[8 * b : 8 * b + 8] for b in range(count)]
    sub = iota((8, width), 0)
    scales = []
    for k in range(count):
        cols = {
            b: [
                jnp.broadcast_to(rows[b][:, 8 * k + j : 8 * k + j + 1], (8, width))
                for j in range(8)
            ]
            for b in range(k, count)
        }
        scale = jnp.zeros((8, width), jnp.float32)
        for j in range(8):
            pivot = jnp.broadcast_to(cols[k][j][j : j + 1], (8, width))
            inverse = 1.0 / pivot
            scale = jnp.where(sub == j, lax.rsqrt(pivot), scale)
            row = jnp.broadcast_to(rows[k][j : j + 1], (8, width))
            heads = [jnp.broadcast_to(cols[k][l][j : j + 1], (8, width)) for l in range(8)]
            for b in range(k, count):
                weight = cols[b][j] * inverse
                if b == k:
                    weight = jnp.where(sub > j, weight, 0.0)
                rows[b] = rows[b] - weight * row
                for l in range(j + 1, 8):
                    cols[b][l] = cols[b][l] - weight * heads[l]
        scales.append(scale)
    scaled = jnp.concatenate([rows[b] * scales[b] for b in range(count)], axis=0)
    return scaled[:, order:]


def leaf_kernel(
    n_outer,
    n_inner,
    pivots_ref,
    front_ref,
    index_ref,
    top_ref,
    panel_out,
    tile_out,
    index_out,
    slab_out,
    columns_out,
    pivot_out,
    work,
    panel_send,
    tile_send,
    slab,
    columns,
    pivot,
    send_sem,
    recv_sem,
    slab_send,
    slab_recv,
    columns_send,
    columns_recv,
    pivot_send,
    pivot_recv,
    local_sem,
):
    outer_index = lax.axis_index("outer")
    inner_index = lax.axis_index("inner")
    leaves = n_outer * n_inner
    flat = outer_index * n_inner + inner_index
    slab_parts, column_parts = slab_recv.shape[0], columns_recv.shape[0]
    slab_rows = slab.shape[0] // slab_parts
    column_rows = columns.shape[0] // column_parts

    def away(offset):
        target = lax.rem(flat + offset, leaves)
        return target, (lax.div(target, n_inner), lax.rem(target, n_inner))

    def remote(source, landing, sent, got, device):
        return pltpu.make_async_remote_copy(
            src_ref=source,
            dst_ref=landing,
            send_sem=sent,
            recv_sem=got,
            device_id=device,
            device_id_type=pl.DeviceIdType.MESH,
        )

    barrier = pltpu.get_barrier_semaphore()

    @pl.loop(1, leaves)
    def _(offset):
        pl.semaphore_signal(
            barrier, inc=1, device_id=away(offset)[1], device_id_type=pl.DeviceIdType.MESH
        )

    pl.semaphore_wait(barrier, leaves - 1)

    def slab_copy(gap, part):
        rows = pl.ds(part * slab_rows, slab_rows)
        level = slab_gaps.index(gap)
        device = (lax.rem(outer_index + gap, n_outer), inner_index)
        return remote(
            slab.at[rows], slab.at[rows], slab_send.at[level, part], slab_recv.at[part], device
        )

    def pivot_copy(gap):
        device = away(gap)[1]
        return remote(pivot, pivot, pivot_send.at[flat_gaps.index(gap)], pivot_recv, device)

    def column_copy(part):
        rows = pl.ds(part * column_rows, column_rows)
        device = (outer_index, lax.rem(inner_index + 1, n_inner))
        return remote(
            columns.at[rows], columns.at[rows], columns_send.at[part], columns_recv.at[part], device
        )

    def halvings(count):
        gaps = []
        while count > 1:
            count //= 2
            gaps.append(count)
        return gaps

    slab_gaps, flat_gaps = halvings(n_outer), halvings(leaves)

    def slab_relay(gap, part):
        @pl.when(lax.rem(outer_index, 2 * gap) == gap)
        def _():
            slab_copy(gap, part).wait_recv()
            for lower in slab_gaps:
                if lower < gap:
                    slab_copy(lower, part).start()

    def pivot_relay(gap):
        @pl.when(lax.rem(flat, 2 * gap) == gap)
        def _():
            pivot_copy(gap).wait_recv()
            for lower in flat_gaps:
                if lower < gap:
                    pivot_copy(lower).start()

    def column_relay(hop, part):
        @pl.when(inner_index == hop)
        def _():
            column_copy(part).wait_recv()
            if hop < n_inner - 1:
                column_copy(part).start()

    local_pivot = pltpu.make_async_copy(
        top_ref.at[pl.ds(0, PIV), pl.ds(0, PIV)], pivot, local_sem.at[0]
    )
    local_slab = pltpu.make_async_copy(top_ref.at[pl.ds(0, PIV), :], slab, local_sem.at[1])
    local_columns = pltpu.make_async_copy(top_ref.at[:, pl.ds(0, PIV)], columns, local_sem.at[2])

    @pl.when(flat == 0)
    def _():
        local_pivot.start()

    @pl.when(outer_index == 0)
    def _():
        local_slab.start()

    @pl.when(inner_index == 0)
    def _():
        local_columns.start()

    def index_copy(offset):
        target, device = away(offset)
        return remote(
            index_ref.at[target],
            index_out.at[flat],
            send_sem.at[2, offset],
            recv_sem.at[2, offset],
            device,
        )

    @pl.when(flat == 0)
    def _():
        local_pivot.wait()
        for gap in flat_gaps:
            pivot_copy(gap).start()

    @pl.when(outer_index == 0)
    def _():
        local_slab.wait()
        for part in range(slab_parts):
            for gap in slab_gaps:
                slab_copy(gap, part).start()

    @pl.when(inner_index == 0)
    def _():
        local_columns.wait()
        for part in range(column_parts):
            column_copy(part).start()

    @pl.loop(1, leaves)
    def _(offset):
        index_copy(offset).start()

    pending = [
        (lambda gap=gap: pivot_relay(gap), order + 1) for order, gap in enumerate(flat_gaps)
    ]
    for hop in range(1, n_inner):
        for part in range(column_parts):
            pending.append((lambda hop=hop, part=part: column_relay(hop, part), hop + part + 0.5))
    for order, gap in enumerate(slab_gaps):
        for part in range(slab_parts):
            pending.append(
                (lambda gap=gap, part=part: slab_relay(gap, part), 2 * order + 2 * part + 2.6)
            )
    pending.sort(key=lambda entry: entry[1])

    def relay(limit):
        while pending and pending[0][1] <= limit:
            pending.pop(0)[0]()

    live = pivots_ref[0]
    row = iota((PV, PV + U), 0)
    col = iota((PV, PV + U), 1)
    keep = (row < live) & ((col < live) | (col >= PV))
    unit = jnp.where((row == col) & (row >= live), 1.0, 0.0)
    work[...] = jnp.where(keep, front_ref[0, :PV, :], unit)
    for start in range(0, PV, NB):
        stop = start + NB
        inverse = inverse_cholesky(work[start:stop, start:stop])
        solved = dot6(inverse, work[start:stop, :])
        work[start:stop, :] = solved
        if stop < PV:
            work[stop:, :] = work[stop:, :] - dot6(solved[:, stop:PV], solved, 0, 0)
            relay(stop // NB)
    coupling = work[:, PV:]
    update = front_ref[0, PV:, PV:] - dot6(coupling, coupling, 0, 0)
    per_row, per_col = U // n_outer, U // n_inner
    half = per_row // 2
    lead = update[:per_row]
    for o in range(n_outer):
        for i in range(n_inner):
            chosen = slice(i * per_col, (i + 1) * per_col)
            panel_send[o * n_inner + i] = jnp.concatenate(
                [
                    lead[:, :per_row],
                    lead[:, chosen],
                    lead[:, o * per_row : (o + 1) * per_row],
                ],
                axis=1,
            )
            first = o * per_row
            tile_send[o * n_inner + i] = jnp.concatenate(
                [
                    update[first : first + half, chosen],
                    update[first + half : first + per_row, chosen],
                ],
                axis=1,
            )

    def panel_copy(offset):
        target, device = away(offset)
        return remote(
            panel_send.at[target],
            panel_out.at[flat],
            send_sem.at[0, offset],
            recv_sem.at[0, offset],
            device,
        )

    def tile_copy(offset):
        target, device = away(offset)
        return remote(
            tile_send.at[target],
            tile_out.at[flat],
            send_sem.at[1, offset],
            recv_sem.at[1, offset],
            device,
        )

    @pl.loop(1, leaves)
    def _(offset):
        panel_copy(offset).start()

    @pl.loop(1, leaves)
    def _(offset):
        tile_copy(offset).start()

    own = [
        pltpu.make_async_copy(panel_send.at[flat], panel_out.at[flat], local_sem.at[3]),
        pltpu.make_async_copy(tile_send.at[flat], tile_out.at[flat], local_sem.at[4]),
        pltpu.make_async_copy(index_ref.at[flat], index_out.at[flat], local_sem.at[5]),
    ]
    for copy in own:
        copy.start()
    relay(1 << 20)
    own.append(pltpu.make_async_copy(slab, slab_out, local_sem.at[6]))
    own.append(pltpu.make_async_copy(columns, columns_out, local_sem.at[7]))
    own.append(pltpu.make_async_copy(pivot, pivot_out, local_sem.at[8]))
    for copy in own[3:]:
        copy.start()

    @pl.loop(1, leaves)
    def _(offset):
        index_copy(offset).wait()
        panel_copy(offset).wait()
        tile_copy(offset).wait()

    for level, gap in enumerate(slab_gaps):
        @pl.when(lax.rem(outer_index, 2 * gap) == 0)
        def _():
            for part in range(slab_parts):
                slab_copy(gap, part).wait_send()

    for gap in flat_gaps:
        @pl.when(lax.rem(flat, 2 * gap) == 0)
        def _():
            pivot_copy(gap).wait_send()

    @pl.when(inner_index < n_inner - 1)
    def _():
        for part in range(column_parts):
            column_copy(part).wait_send()

    for copy in own:
        copy.wait()


def panel_kernel(
    shape,
    panel_ref,
    index_ref,
    pivot_ref,
    slab_ref,
    columns_ref,
    factor_ref,
    slab_factor_ref,
    e_pivot,
    e_slab,
    e_row,
    lead_sub,
    row_sub,
    col_sub,
):
    leaves, per_row, per_col, tile_rows, tile_cols = shape
    turned = index_ref[...].astype(jnp.float32).T.astype(jnp.int32)
    for d in range(leaves):
        lanes = index_ref[d : d + 1, :per_row]
        lead_sub[d * per_row : (d + 1) * per_row, :] = turned[:per_row, d : d + 1]
        col_sub[d * per_col : (d + 1) * per_col, :] = turned[per_row : per_row + per_col, d : d + 1]
        row_sub[d * per_row : (d + 1) * per_row, :] = turned[per_row + per_col :, d : d + 1]
        pick = (iota((PIV, per_row), 0) == lanes).astype(jnp.bfloat16)
        high, low = halves(panel_ref[d])
        spread = dot(pick, high) + dot(pick, low)
        e_pivot[:, d * per_row : (d + 1) * per_row] = spread[:, :per_row]
        e_slab[:, d * per_col : (d + 1) * per_col] = spread[:, per_row : per_row + per_col]
        e_row[:, d * per_row : (d + 1) * per_row] = spread[:, per_row + per_col :]

    def place(source, index_ref, width):
        depth = source.shape[1]
        pick = (iota((depth, width), 1) == index_ref[...]).astype(jnp.bfloat16)
        high, low = halves(source)
        return dot(high, pick) + dot(low, pick)

    pivot = pivot_ref[...] + place(e_pivot[...], lead_sub, PIV)
    first = inverse_cholesky(pivot[:NB, :NB])
    across = dot6(first, pivot[:NB, NB:])
    second = inverse_cholesky(pivot[NB:, NB:] - dot6(across, across, 0, 0))
    below = -dot6(second, dot6(across, first, 0, 0))
    inverse = jnp.concatenate(
        [
            jnp.concatenate([first, jnp.zeros_like(first)], axis=1),
            jnp.concatenate([below, second], axis=1),
        ],
        axis=0,
    )
    width = min(tile_cols, 512)
    for start in range(0, tile_cols, width):
        pick = (iota((leaves * per_col, width), 1) + start == col_sub[...]).astype(jnp.bfloat16)
        high, low = halves(e_slab[...])
        part = slab_ref[:, start : start + width] + (dot(high, pick) + dot(low, pick))
        slab_factor_ref[:, start : start + width] = dot3(inverse, part)
    width = min(tile_rows, 512)
    for start in range(0, tile_rows, width):
        pick = (iota((leaves * per_row, width), 1) + start == row_sub[...]).astype(jnp.bfloat16)
        high, low = halves(e_row[...])
        part = columns_ref[start : start + width, :].T + (dot(high, pick) + dot(low, pick))
        factor_ref[start : start + width, :] = dot3(inverse, part).T

    outer_index = lax.axis_index("outer")

    @pl.when(outer_index * tile_rows < PIV)
    def _():
        for start in range(0, tile_rows, 128):
            span = min(128, tile_rows - start)
            rows = outer_index * tile_rows + start + iota((span, PIV), 0)
            block = factor_ref[start : start + span, :]
            factor_ref[start : start + span, :] = jnp.where(
                rows >= iota((span, PIV), 1), block, 0.0
            )


def trailing_kernel(
    shape,
    tile_ref,
    index_ref,
    top_ref,
    factor_ref,
    slab_ref,
    schur_ref,
    high_ref,
    low_ref,
    row_lane,
):
    leaves, per_row, per_col, tile_rows, tile_cols = shape
    step = pl.program_id(0)
    height = top_ref.shape[0]
    half = per_row // 2

    @pl.when(step == 0)
    def _():
        turned = index_ref[...].astype(jnp.float32).T.astype(jnp.int32)
        for d in range(leaves):
            row_lane[:, d * per_row : (d + 1) * per_row] = index_ref[
                d : d + 1, per_row + per_col :
            ]
            packed = tile_ref[d]
            values = jnp.concatenate([packed[:, :per_col], packed[:, per_col:]], axis=0)
            pick = (
                iota((per_col, tile_cols), 1) == turned[per_row : per_row + per_col, d : d + 1]
            ).astype(jnp.bfloat16)
            high, low = halves(values)
            spread = dot(high, pick)
            spread_low = dot(low, pick)
            high_ref[d * per_row : (d + 1) * per_row, :] = spread.astype(jnp.bfloat16)
            low_ref[d * per_row : (d + 1) * per_row, :] = spread_low.astype(jnp.bfloat16)

    rows = step * height + iota((height, leaves * per_row), 0)
    pick = (rows == row_lane[...]).astype(jnp.bfloat16)
    f_high, f_low = halves(-factor_ref[...])
    width = min(tile_cols, 512)
    row_global = lax.axis_index("outer") * tile_rows + step * height + iota((height, width), 0)
    for start in range(0, tile_cols, width):
        cols = slice(start, start + width)
        s_high, s_low = halves(slab_ref[:, cols])
        total = dot(pick, high_ref[:, cols]) + dot(pick, low_ref[:, cols])
        total = total + (dot(f_high, s_high) + (dot(f_high, s_low) + dot(f_low, s_high)))
        col_global = lax.axis_index("inner") * tile_cols + start + iota((height, width), 1)
        keep = (row_global >= PIV) & (col_global >= PIV)
        schur_ref[:, cols] = jnp.where(keep, top_ref[:, cols] + total, 0.0)


def shards(leaf_fronts, pivot_count, update_rows, top_front):
    n_outer = lax.axis_size("outer")
    n_inner = lax.axis_size("inner")
    tile_rows, tile_cols = top_front.shape
    leaves = n_outer * n_inner
    per_row, per_col = U // n_outer, U // n_inner
    shape = (leaves, per_row, per_col, tile_rows, tile_cols)
    vmem = pl.BlockSpec(memory_space=pltpu.VMEM)
    big = pltpu.CompilerParams(vmem_limit_bytes=56 << 20)

    lead = update_rows[0, :per_row]
    rows = (update_rows[0] % tile_rows).reshape(n_outer, 1, per_row)
    cols = (update_rows[0] % tile_cols).reshape(1, n_inner, per_col)
    grid = (n_outer, n_inner)
    messages = jnp.concatenate(
        [
            jnp.broadcast_to(lead, grid + (per_row,)),
            jnp.broadcast_to(cols, grid + (per_col,)),
            jnp.broadcast_to(rows, grid + (per_row,)),
        ],
        axis=2,
    )
    lanes = 2 * per_row + per_col
    messages = messages.reshape(leaves, 1, lanes)

    levels = (n_outer - 1).bit_length()
    slab_parts, column_parts = 2, 4
    anywhere = pl.BlockSpec(memory_space=pl.ANY)
    dma = pltpu.SemaphoreType.DMA
    real = lambda *dims: jax.ShapeDtypeStruct(dims, jnp.float32)
    panel, tiles, indices, slab, columns, pivot_raw = pl.pallas_call(
        functools.partial(leaf_kernel, n_outer, n_inner),
        out_shape=(
            real(leaves, per_row, lanes),
            real(leaves, per_row // 2, 2 * per_col),
            jax.ShapeDtypeStruct((leaves, 1, lanes), jnp.int32),
            real(PIV, tile_cols),
            real(tile_rows, PIV),
            real(PIV, PIV),
        ),
        in_specs=[pl.BlockSpec(memory_space=pltpu.SMEM), vmem, vmem, anywhere],
        out_specs=(anywhere,) * 6,
        scratch_shapes=[
            pltpu.VMEM((PV, PV + U), jnp.float32),
            pltpu.VMEM((leaves, per_row, lanes), jnp.float32),
            pltpu.VMEM((leaves, per_row // 2, 2 * per_col), jnp.float32),
            pltpu.VMEM((PIV, tile_cols), jnp.float32),
            pltpu.VMEM((tile_rows, PIV), jnp.float32),
            pltpu.VMEM((PIV, PIV), jnp.float32),
            dma((3, leaves)),
            dma((3, leaves)),
            dma((levels, slab_parts)),
            dma((slab_parts,)),
            dma((column_parts,)),
            dma((column_parts,)),
            dma(((leaves - 1).bit_length(),)),
            dma,
            dma((9,)),
        ],
        compiler_params=pltpu.CompilerParams(
            vmem_limit_bytes=56 << 20, collective_id=0, has_side_effects=True
        ),
    )(pivot_count, leaf_fronts, messages, top_front)
    indices = indices.reshape(leaves, lanes)

    factor, slab_factor = pl.pallas_call(
        functools.partial(panel_kernel, shape),
        out_shape=(real(tile_rows, PIV), real(PIV, tile_cols)),
        in_specs=[vmem] * 5,
        out_specs=(vmem, vmem),
        scratch_shapes=[
            pltpu.VMEM((PIV, leaves * per_row), jnp.float32),
            pltpu.VMEM((PIV, leaves * per_col), jnp.float32),
            pltpu.VMEM((PIV, leaves * per_row), jnp.float32),
            pltpu.VMEM((leaves * per_row, 1), jnp.int32),
            pltpu.VMEM((leaves * per_row, 1), jnp.int32),
            pltpu.VMEM((leaves * per_col, 1), jnp.int32),
        ],
        compiler_params=big,
    )(panel, indices, pivot_raw, slab, columns)

    height = min(tile_rows, 128)
    whole = lambda *dims: pl.BlockSpec(dims, lambda r: (0,) * len(dims))
    schur = pl.pallas_call(
        functools.partial(trailing_kernel, shape),
        out_shape=jax.ShapeDtypeStruct((tile_rows, tile_cols), jnp.float32),
        grid=(tile_rows // height,),
        in_specs=[
            whole(leaves, per_row // 2, 2 * per_col),
            whole(leaves, lanes),
            pl.BlockSpec((height, tile_cols), lambda r: (r, 0)),
            pl.BlockSpec((height, PIV), lambda r: (r, 0)),
            whole(PIV, tile_cols),
        ],
        out_specs=pl.BlockSpec((height, tile_cols), lambda r: (r, 0)),
        scratch_shapes=[
            pltpu.VMEM((leaves * per_row, tile_cols), jnp.bfloat16),
            pltpu.VMEM((leaves * per_row, tile_cols), jnp.bfloat16),
            pltpu.VMEM((1, leaves * per_row), jnp.int32),
        ],
        compiler_params=big,
    )(tiles, indices, top_front, factor, slab_factor)
    return (factor, schur)


def solution(mesh):
    placed = (
        P(("outer", "inner"), None, None),
        P(("outer", "inner")),
        P(("outer", "inner"), None),
        P("outer", "inner"),
    )
    return jax.shard_map(
        shards,
        mesh=mesh,
        in_specs=placed,
        out_specs=(P("outer", None), P("outer", "inner")),
        check_vma=False,
    )
```

```python
import functools

import jax
import jax.numpy as jnp
from jax import lax
from jax.experimental import pallas as pl
from jax.experimental.pallas import tpu as pltpu
from jax.sharding import PartitionSpec as P

PV = 256
U = 256
PIV = 128
NB = 64


def iota(shape, dim):
    return lax.broadcasted_iota(jnp.int32, shape, dim)


def dot(a, b, ca=1, cb=0):
    return lax.dot_general(
        a, b, (((ca,), (cb,)), ((), ())), preferred_element_type=jnp.float32
    )


def halves(x):
    high = x.astype(jnp.bfloat16)
    return high, (x - high.astype(jnp.float32)).astype(jnp.bfloat16)


def dot3(a, b, ca=1, cb=0):
    a_high, a_low = halves(a)
    b_high, b_low = halves(b)
    return dot(a_high, b_high, ca, cb) + (dot(a_high, b_low, ca, cb) + dot(a_low, b_high, ca, cb))


def dot6(a, b, ca=1, cb=0):
    return lax.dot_general(
        a,
        b,
        (((ca,), (cb,)), ((), ())),
        precision=lax.Precision.HIGHEST,
        preferred_element_type=jnp.float32,
    )


def inverse_cholesky(block):
    order = block.shape[0]
    unit = (iota((order, order), 0) == iota((order, order), 1)).astype(jnp.float32)
    joined = jnp.concatenate([block, unit], axis=1)
    width = joined.shape[1]
    count = order // 8
    rows = [joined[8 * b : 8 * b + 8] for b in range(count)]
    sub = iota((8, width), 0)
    scales = []
    for k in range(count):
        cols = {
            b: [
                jnp.broadcast_to(rows[b][:, 8 * k + j : 8 * k + j + 1], (8, width))
                for j in range(8)
            ]
            for b in range(k, count)
        }
        scale = jnp.zeros((8, width), jnp.float32)
        for j in range(8):
            pivot = jnp.broadcast_to(cols[k][j][j : j + 1], (8, width))
            inverse = 1.0 / pivot
            scale = jnp.where(sub == j, lax.rsqrt(pivot), scale)
            row = jnp.broadcast_to(rows[k][j : j + 1], (8, width))
            heads = [jnp.broadcast_to(cols[k][l][j : j + 1], (8, width)) for l in range(8)]
            for b in range(k, count):
                weight = cols[b][j] * inverse
                if b == k:
                    weight = jnp.where(sub > j, weight, 0.0)
                rows[b] = rows[b] - weight * row
                for l in range(j + 1, 8):
                    cols[b][l] = cols[b][l] - weight * heads[l]
        scales.append(scale)
    scaled = jnp.concatenate([rows[b] * scales[b] for b in range(count)], axis=0)
    return scaled[:, order:]


def leaf_kernel(
    n_outer,
    n_inner,
    pivots_ref,
    front_ref,
    index_ref,
    top_ref,
    panel_out,
    tile_ref,
    index_out,
    slab_out,
    columns_out,
    pivot_out,
    work,
    panel_send,
    index_send,
    slab,
    columns,
    pivot,
    send_sem,
    recv_sem,
    slab_send,
    slab_recv,
    columns_send,
    columns_recv,
    pivot_send,
    pivot_recv,
    local_sem,
):
    outer_index = lax.axis_index("outer")
    inner_index = lax.axis_index("inner")
    leaves = n_outer * n_inner
    flat = outer_index * n_inner + inner_index
    slab_parts, column_parts = slab_recv.shape[0], columns_recv.shape[0]
    slab_rows = slab.shape[0] // slab_parts
    column_rows = columns.shape[0] // column_parts

    def away(offset):
        target = lax.rem(flat + offset, leaves)
        return target, (lax.div(target, n_inner), lax.rem(target, n_inner))

    def remote(source, landing, sent, got, device):
        return pltpu.make_async_remote_copy(
            src_ref=source,
            dst_ref=landing,
            send_sem=sent,
            recv_sem=got,
            device_id=device,
            device_id_type=pl.DeviceIdType.MESH,
        )

    barrier = pltpu.get_barrier_semaphore()

    @pl.loop(1, leaves)
    def _(offset):
        pl.semaphore_signal(
            barrier, inc=1, device_id=away(offset)[1], device_id_type=pl.DeviceIdType.MESH
        )

    pl.semaphore_wait(barrier, leaves - 1)

    def slab_copy(gap, part):
        rows = pl.ds(part * slab_rows, slab_rows)
        level = slab_gaps.index(gap)
        device = (lax.rem(outer_index + gap, n_outer), inner_index)
        return remote(
            slab.at[rows], slab.at[rows], slab_send.at[level, part], slab_recv.at[part], device
        )

    def pivot_copy(gap):
        device = away(gap)[1]
        return remote(pivot, pivot, pivot_send.at[flat_gaps.index(gap)], pivot_recv, device)

    def column_copy(part):
        rows = pl.ds(part * column_rows, column_rows)
        device = (outer_index, lax.rem(inner_index + 1, n_inner))
        return remote(
            columns.at[rows], columns.at[rows], columns_send.at[part], columns_recv.at[part], device
        )

    def halvings(count):
        gaps = []
        while count > 1:
            count //= 2
            gaps.append(count)
        return gaps

    slab_gaps, flat_gaps = halvings(n_outer), halvings(leaves)

    def slab_relay(gap, part):
        @pl.when(lax.rem(outer_index, 2 * gap) == gap)
        def _():
            slab_copy(gap, part).wait_recv()
            for lower in slab_gaps:
                if lower < gap:
                    slab_copy(lower, part).start()

    def pivot_relay(gap):
        @pl.when(lax.rem(flat, 2 * gap) == gap)
        def _():
            pivot_copy(gap).wait_recv()
            for lower in flat_gaps:
                if lower < gap:
                    pivot_copy(lower).start()

    def column_relay(hop, part):
        @pl.when(inner_index == hop)
        def _():
            column_copy(part).wait_recv()
            if hop < n_inner - 1:
                column_copy(part).start()

    local_pivot = pltpu.make_async_copy(
        top_ref.at[pl.ds(0, PIV), pl.ds(0, PIV)], pivot, local_sem.at[0]
    )
    local_slab = pltpu.make_async_copy(top_ref.at[pl.ds(0, PIV), :], slab, local_sem.at[1])
    local_columns = pltpu.make_async_copy(top_ref.at[:, pl.ds(0, PIV)], columns, local_sem.at[2])

    @pl.when(flat == 0)
    def _():
        local_pivot.start()

    @pl.when(outer_index == 0)
    def _():
        local_slab.start()

    @pl.when(inner_index == 0)
    def _():
        local_columns.start()

    def index_copy(offset):
        target, device = away(offset)
        return remote(
            index_send.at[target],
            index_out.at[flat],
            send_sem.at[1, offset],
            recv_sem.at[1, offset],
            device,
        )

    @pl.when(flat == 0)
    def _():
        local_pivot.wait()
        for gap in flat_gaps:
            pivot_copy(gap).start()

    @pl.when(outer_index == 0)
    def _():
        local_slab.wait()
        for part in range(slab_parts):
            for gap in slab_gaps:
                slab_copy(gap, part).start()

    @pl.when(inner_index == 0)
    def _():
        local_columns.wait()
        for part in range(column_parts):
            column_copy(part).start()

    per_row, per_col = U // n_outer, U // n_inner
    tile_rows, tile_cols = top_ref.shape
    targets = index_ref[...]
    for o in range(n_outer):
        for i in range(n_inner):
            index_send[o * n_inner + i] = jnp.concatenate(
                [
                    targets[:, :per_row],
                    targets[:, i * per_col : (i + 1) * per_col] - i * tile_cols,
                    targets[:, o * per_row : (o + 1) * per_row] - o * tile_rows,
                ],
                axis=1,
            )

    @pl.loop(1, leaves)
    def _(offset):
        index_copy(offset).start()

    pending = [
        (lambda gap=gap: pivot_relay(gap), order + 1) for order, gap in enumerate(flat_gaps)
    ]
    for hop in range(1, n_inner):
        for part in range(column_parts):
            pending.append((lambda hop=hop, part=part: column_relay(hop, part), hop + part + 0.5))
    for order, gap in enumerate(slab_gaps):
        for part in range(slab_parts):
            pending.append(
                (lambda gap=gap, part=part: slab_relay(gap, part), 2 * order + 2 * part + 2.6)
            )
    pending.sort(key=lambda entry: entry[1])

    def relay(limit):
        while pending and pending[0][1] <= limit:
            pending.pop(0)[0]()

    live = pivots_ref[0]
    row = iota((PV, PV + U), 0)
    col = iota((PV, PV + U), 1)
    keep = (row < live) & ((col < live) | (col >= PV))
    unit = jnp.where((row == col) & (row >= live), 1.0, 0.0)
    work[...] = jnp.where(keep, front_ref[0, :PV, :], unit)
    for start in range(0, PV, NB):
        stop = start + NB
        inverse = inverse_cholesky(work[start:stop, start:stop])
        solved = dot6(inverse, work[start:stop, :])
        work[start:stop, :] = solved
        if stop < PV:
            work[stop:, :] = work[stop:, :] - dot6(solved[:, stop:PV], solved, 0, 0)
            relay(stop // NB)
    coupling = work[:, PV:]
    update = front_ref[0, PV:, PV:] - dot6(coupling, coupling, 0, 0)
    half = per_row // 2
    lead = update[:per_row]
    for o in range(n_outer):
        for i in range(n_inner):
            chosen = slice(i * per_col, (i + 1) * per_col)
            panel_send[o * n_inner + i] = jnp.concatenate(
                [
                    lead[:, :per_row],
                    lead[:, chosen],
                    lead[:, o * per_row : (o + 1) * per_row],
                ],
                axis=1,
            )
            first = o * per_row
            tile_ref[o * n_inner + i] = jnp.concatenate(
                [
                    update[first : first + half, chosen],
                    update[first + half : first + per_row, chosen],
                ],
                axis=1,
            )

    def panel_copy(offset):
        target, device = away(offset)
        return remote(
            panel_send.at[target],
            panel_out.at[flat],
            send_sem.at[0, offset],
            recv_sem.at[0, offset],
            device,
        )

    relay(4)

    @pl.loop(1, leaves)
    def _(offset):
        panel_copy(offset).start()

    own = [
        pltpu.make_async_copy(panel_send.at[flat], panel_out.at[flat], local_sem.at[3]),
        pltpu.make_async_copy(index_send.at[flat], index_out.at[flat], local_sem.at[4]),
    ]
    for copy in own:
        copy.start()
    relay(1 << 20)
    own.append(pltpu.make_async_copy(slab, slab_out, local_sem.at[5]))
    own.append(pltpu.make_async_copy(columns, columns_out, local_sem.at[6]))
    own.append(pltpu.make_async_copy(pivot, pivot_out, local_sem.at[7]))
    for copy in own[2:]:
        copy.start()

    @pl.loop(1, leaves)
    def _(offset):
        index_copy(offset).wait()
        panel_copy(offset).wait()

    for level, gap in enumerate(slab_gaps):
        @pl.when(lax.rem(outer_index, 2 * gap) == 0)
        def _():
            for part in range(slab_parts):
                slab_copy(gap, part).wait_send()

    for gap in flat_gaps:
        @pl.when(lax.rem(flat, 2 * gap) == 0)
        def _():
            pivot_copy(gap).wait_send()

    @pl.when(inner_index < n_inner - 1)
    def _():
        for part in range(column_parts):
            column_copy(part).wait_send()

    for copy in own:
        copy.wait()


def panel_kernel(
    shape,
    n_inner,
    panel_ref,
    index_ref,
    pivot_ref,
    slab_ref,
    columns_ref,
    tile_ref,
    factor_ref,
    slab_factor_ref,
    tile_out,
    e_pivot,
    e_slab,
    e_row,
    lead_sub,
    row_sub,
    col_sub,
    send_sem,
    recv_sem,
    local_sem,
):
    leaves, per_row, per_col, tile_rows, tile_cols = shape
    outer_index = lax.axis_index("outer")
    flat = outer_index * n_inner + lax.axis_index("inner")

    def away(offset):
        target = lax.rem(flat + offset, leaves)
        return target, (lax.div(target, n_inner), lax.rem(target, n_inner))

    def tile_copy(offset):
        target, device = away(offset)
        return pltpu.make_async_remote_copy(
            src_ref=tile_ref.at[target],
            dst_ref=tile_out.at[flat],
            send_sem=send_sem.at[offset],
            recv_sem=recv_sem.at[offset],
            device_id=device,
            device_id_type=pl.DeviceIdType.MESH,
        )

    barrier = pltpu.get_barrier_semaphore()

    @pl.loop(1, leaves)
    def _(offset):
        pl.semaphore_signal(
            barrier, inc=1, device_id=away(offset)[1], device_id_type=pl.DeviceIdType.MESH
        )

    own = pltpu.make_async_copy(tile_ref.at[flat], tile_out.at[flat], local_sem)
    own.start()
    turned = index_ref[...].astype(jnp.float32).T.astype(jnp.int32)
    for d in range(leaves):
        lanes = index_ref[d : d + 1, :per_row]
        lead_sub[d * per_row : (d + 1) * per_row, :] = turned[:per_row, d : d + 1]
        col_sub[d * per_col : (d + 1) * per_col, :] = turned[per_row : per_row + per_col, d : d + 1]
        row_sub[d * per_row : (d + 1) * per_row, :] = turned[per_row + per_col :, d : d + 1]
        pick = (iota((PIV, per_row), 0) == lanes).astype(jnp.bfloat16)
        high, low = halves(panel_ref[d])
        spread = dot(pick, high) + dot(pick, low)
        e_pivot[:, d * per_row : (d + 1) * per_row] = spread[:, :per_row]
        e_slab[:, d * per_col : (d + 1) * per_col] = spread[:, per_row : per_row + per_col]
        e_row[:, d * per_row : (d + 1) * per_row] = spread[:, per_row + per_col :]

    def place(source, index_ref, width):
        depth = source.shape[1]
        pick = (iota((depth, width), 1) == index_ref[...]).astype(jnp.bfloat16)
        high, low = halves(source)
        return dot(high, pick) + dot(low, pick)

    pivot = pivot_ref[...] + place(e_pivot[...], lead_sub, PIV)
    first = inverse_cholesky(pivot[:NB, :NB])
    across = dot6(first, pivot[:NB, NB:])
    second = inverse_cholesky(pivot[NB:, NB:] - dot6(across, across, 0, 0))
    below = -dot6(second, dot6(across, first, 0, 0))
    inverse = jnp.concatenate(
        [
            jnp.concatenate([first, jnp.zeros_like(first)], axis=1),
            jnp.concatenate([below, second], axis=1),
        ],
        axis=0,
    )
    pl.semaphore_wait(barrier, leaves - 1)

    @pl.loop(1, leaves)
    def _(offset):
        tile_copy(offset).start()

    width = min(tile_cols, 512)
    for start in range(0, tile_cols, width):
        pick = (iota((leaves * per_col, width), 1) + start == col_sub[...]).astype(jnp.bfloat16)
        high, low = halves(e_slab[...])
        part = slab_ref[:, start : start + width] + (dot(high, pick) + dot(low, pick))
        slab_factor_ref[:, start : start + width] = dot3(inverse, part)
    width = min(tile_rows, 512)
    for start in range(0, tile_rows, width):
        pick = (iota((leaves * per_row, width), 1) + start == row_sub[...]).astype(jnp.bfloat16)
        high, low = halves(e_row[...])
        part = columns_ref[start : start + width, :].T + (dot(high, pick) + dot(low, pick))
        factor_ref[start : start + width, :] = dot3(inverse, part).T

    @pl.when(outer_index * tile_rows < PIV)
    def _():
        for start in range(0, tile_rows, 128):
            span = min(128, tile_rows - start)
            rows = outer_index * tile_rows + start + iota((span, PIV), 0)
            block = factor_ref[start : start + span, :]
            factor_ref[start : start + span, :] = jnp.where(
                rows >= iota((span, PIV), 1), block, 0.0
            )

    @pl.loop(1, leaves)
    def _(offset):
        tile_copy(offset).wait()

    own.wait()


def trailing_kernel(
    shape,
    tile_ref,
    index_ref,
    top_ref,
    factor_ref,
    slab_ref,
    schur_ref,
    high_ref,
    low_ref,
    row_lane,
):
    leaves, per_row, per_col, tile_rows, tile_cols = shape
    step = pl.program_id(0)
    height = top_ref.shape[0]
    half = per_row // 2

    @pl.when(step == 0)
    def _():
        turned = index_ref[...].astype(jnp.float32).T.astype(jnp.int32)
        for d in range(leaves):
            row_lane[:, d * per_row : (d + 1) * per_row] = index_ref[
                d : d + 1, per_row + per_col :
            ]
            packed = tile_ref[d]
            values = jnp.concatenate([packed[:, :per_col], packed[:, per_col:]], axis=0)
            pick = (
                iota((per_col, tile_cols), 1) == turned[per_row : per_row + per_col, d : d + 1]
            ).astype(jnp.bfloat16)
            high, low = halves(values)
            spread = dot(high, pick)
            spread_low = dot(low, pick)
            high_ref[d * per_row : (d + 1) * per_row, :] = spread.astype(jnp.bfloat16)
            low_ref[d * per_row : (d + 1) * per_row, :] = spread_low.astype(jnp.bfloat16)

    rows = step * height + iota((height, leaves * per_row), 0)
    pick = (rows == row_lane[...]).astype(jnp.bfloat16)
    f_high, f_low = halves(-factor_ref[...])
    width = min(tile_cols, 512)
    row_global = lax.axis_index("outer") * tile_rows + step * height + iota((height, width), 0)
    for start in range(0, tile_cols, width):
        cols = slice(start, start + width)
        s_high, s_low = halves(slab_ref[:, cols])
        total = dot(pick, high_ref[:, cols]) + dot(pick, low_ref[:, cols])
        total = total + (dot(f_high, s_high) + (dot(f_high, s_low) + dot(f_low, s_high)))
        col_global = lax.axis_index("inner") * tile_cols + start + iota((height, width), 1)
        keep = (row_global >= PIV) & (col_global >= PIV)
        schur_ref[:, cols] = jnp.where(keep, top_ref[:, cols] + total, 0.0)


def shards(leaf_fronts, pivot_count, update_rows, top_front):
    n_outer = lax.axis_size("outer")
    n_inner = lax.axis_size("inner")
    tile_rows, tile_cols = top_front.shape
    leaves = n_outer * n_inner
    per_row, per_col = U // n_outer, U // n_inner
    shape = (leaves, per_row, per_col, tile_rows, tile_cols)
    vmem = pl.BlockSpec(memory_space=pltpu.VMEM)
    big = pltpu.CompilerParams(vmem_limit_bytes=56 << 20)

    lanes = 2 * per_row + per_col

    levels = (n_outer - 1).bit_length()
    slab_parts, column_parts = 2, 4
    anywhere = pl.BlockSpec(memory_space=pl.ANY)
    dma = pltpu.SemaphoreType.DMA
    real = lambda *dims: jax.ShapeDtypeStruct(dims, jnp.float32)
    panel, tiles, indices, slab, columns, pivot_raw = pl.pallas_call(
        functools.partial(leaf_kernel, n_outer, n_inner),
        out_shape=(
            real(leaves, per_row, lanes),
            real(leaves, per_row // 2, 2 * per_col),
            jax.ShapeDtypeStruct((leaves, 1, lanes), jnp.int32),
            real(PIV, tile_cols),
            real(tile_rows, PIV),
            real(PIV, PIV),
        ),
        in_specs=[pl.BlockSpec(memory_space=pltpu.SMEM), vmem, vmem, anywhere],
        out_specs=(anywhere, vmem) + (anywhere,) * 4,
        scratch_shapes=[
            pltpu.VMEM((PV, PV + U), jnp.float32),
            pltpu.VMEM((leaves, per_row, lanes), jnp.float32),
            pltpu.VMEM((leaves, 1, lanes), jnp.int32),
            pltpu.VMEM((PIV, tile_cols), jnp.float32),
            pltpu.VMEM((tile_rows, PIV), jnp.float32),
            pltpu.VMEM((PIV, PIV), jnp.float32),
            dma((2, leaves)),
            dma((2, leaves)),
            dma((levels, slab_parts)),
            dma((slab_parts,)),
            dma((column_parts,)),
            dma((column_parts,)),
            dma(((leaves - 1).bit_length(),)),
            dma,
            dma((8,)),
        ],
        compiler_params=pltpu.CompilerParams(
            vmem_limit_bytes=56 << 20, collective_id=0, has_side_effects=True
        ),
    )(pivot_count, leaf_fronts, update_rows, top_front)
    indices = indices.reshape(leaves, lanes)

    factor, slab_factor, tiles = pl.pallas_call(
        functools.partial(panel_kernel, shape, n_inner),
        out_shape=(
            real(tile_rows, PIV),
            real(PIV, tile_cols),
            real(leaves, per_row // 2, 2 * per_col),
        ),
        in_specs=[vmem] * 5 + [anywhere],
        out_specs=(vmem, vmem, anywhere),
        scratch_shapes=[
            pltpu.VMEM((PIV, leaves * per_row), jnp.float32),
            pltpu.VMEM((PIV, leaves * per_col), jnp.float32),
            pltpu.VMEM((PIV, leaves * per_row), jnp.float32),
            pltpu.VMEM((leaves * per_row, 1), jnp.int32),
            pltpu.VMEM((leaves * per_row, 1), jnp.int32),
            pltpu.VMEM((leaves * per_col, 1), jnp.int32),
            dma((leaves,)),
            dma((leaves,)),
            dma,
        ],
        compiler_params=pltpu.CompilerParams(
            vmem_limit_bytes=56 << 20, collective_id=1, has_side_effects=True
        ),
    )(panel, indices, pivot_raw, slab, columns, tiles)

    height = min(tile_rows, 256)
    whole = lambda *dims: pl.BlockSpec(dims, lambda r: (0,) * len(dims))
    schur = pl.pallas_call(
        functools.partial(trailing_kernel, shape),
        out_shape=jax.ShapeDtypeStruct((tile_rows, tile_cols), jnp.float32),
        grid=(tile_rows // height,),
        in_specs=[
            whole(leaves, per_row // 2, 2 * per_col),
            whole(leaves, lanes),
            pl.BlockSpec((height, tile_cols), lambda r: (r, 0)),
            pl.BlockSpec((height, PIV), lambda r: (r, 0)),
            whole(PIV, tile_cols),
        ],
        out_specs=pl.BlockSpec((height, tile_cols), lambda r: (r, 0)),
        scratch_shapes=[
            pltpu.VMEM((leaves * per_row, tile_cols), jnp.bfloat16),
            pltpu.VMEM((leaves * per_row, tile_cols), jnp.bfloat16),
            pltpu.VMEM((1, leaves * per_row), jnp.int32),
        ],
        compiler_params=big,
    )(tiles, indices, top_front, factor, slab_factor)
    return (factor, schur)


def solution(mesh):
    placed = (
        P(("outer", "inner"), None, None),
        P(("outer", "inner")),
        P(("outer", "inner"), None),
        P("outer", "inner"),
    )
    return jax.shard_map(
        shards,
        mesh=mesh,
        in_specs=placed,
        out_specs=(P("outer", None), P("outer", "inner")),
        check_vma=False,
    )
```
